128 devices in a mesh: aux: 8 (over y_hi, z), occ: 16 (over y_lo, x, core).
Axes of the slice: x: 4, y: 4 (y_hi: 2, y_lo: 2; y = y_hi * 2 + y_lo), z: 4, core: 2. Of those that a mesh axis runs over, the one named last changes fastest.
Arguments:
- half_ints: bfloat16 [1024, 512, 1024], P('aux', 'occ'), may hold values from -1 to 1
- block_mask: int32 [16, 512], P('aux', 'occ'), may hold values 0 or 1
- vir_coef: bfloat16 [1024, 2048], replicated, may hold values from -0.1875 to 0.1875
- domains: int32 [512, 512], replicated, may hold values from 0 to 2047, as said below
- vir_energy: float32 [2048], replicated, may hold values from 0.5 to 3
- occ_energy: float32 [512], replicated, may hold values from -3 to -0.5
- pair_count: int32 [16, 8], P('occ', 'aux'), may hold values from 2 to 16, as said below
- pair_code: int32 [16, 8, 16], P('occ', 'aux'), may hold values from 0 to 63, as said below
Outputs:
- density: bfloat16 [1024, 512, 512], P('aux', 'occ')
The draws below stay inside these ranges and needn't reach their ends.
Inputs may be any that keep to these rules, and one draw needn't show every extreme that they name: `domains`: each row names 512 distinct virtual orbitals. `pair_count`: some block holds exactly 16 live pairs. `pair_code`: the entries of one block's list are distinct.
All inputs are finite; a program needn't handle non-finite values. No bound on the sum of `block_mask` on one device may be relied on, other than what follows from the above.
Results may differ from the reference program's by a relative error of at most 0.0075.
Values may be sent and summed in bfloat16 or wider, within the bound.
A program may use at most 128 MiB of HBM per device.

```python
import jax
import jax.numpy as jnp
from jax import lax

AUX = 1024
NVIR = 512
NBAS = 1024
NVALL = 2048
BLK = 64
OCC_DEV = 4
PARTNERS = 4
PAIR_CAP = 16
NOCC = 512
NBLK = 16
OCC_GROUPS = 16
AUX_GROUPS = 8
N_AUX = 8
N_OCC = 16


def draw_domains(key, part):
    keys = jax.random.split(jax.random.fold_in(key, 31), NOCC)

    def one_row(row_key):
        return jax.random.permutation(row_key, NVALL)[:NVIR]
    return jax.vmap(one_row)(keys).astype(jnp.int32)


def draw_pair_count(key, part):
    first = jax.random.fold_in(key, 11)
    second = jax.random.fold_in(key, 12)
    draws = jax.random.randint(first, (OCC_GROUPS * AUX_GROUPS,), 0, PAIR_CAP)
    counts = jnp.minimum(2 + draws * draws // PAIR_CAP, PAIR_CAP)
    chosen = jax.random.randint(second, (), 0, OCC_GROUPS * AUX_GROUPS)
    counts = counts.at[chosen].set(PAIR_CAP)
    return counts.reshape(OCC_GROUPS, AUX_GROUPS).astype(jnp.int32)


def draw_pair_code(key, part):
    keys = jax.random.split(jax.random.fold_in(key, 21), OCC_GROUPS * AUX_GROUPS)

    def one_list(list_key):
        return jax.random.permutation(list_key, PARTNERS * OCC_DEV * OCC_DEV)[:PAIR_CAP]
    codes = jax.vmap(one_list)(keys)
    return codes.reshape(OCC_GROUPS, AUX_GROUPS, PAIR_CAP).astype(jnp.int32)


def touch_ends(drawn, stream_key, least, high):
    dims = drawn.shape
    spot = [jax.random.randint(jax.random.fold_in(stream_key, axis), (), 0, dims[axis]) for axis in range(len(dims))]
    drawn = drawn.at[tuple(spot)].set(least)
    longest = dims.index(max(dims))
    spot[longest] = (spot[longest] + 1) % dims[longest]
    return drawn.at[tuple(spot)].set(high)


def block_scale(own_key, dims, pieces, least, largest):
    loudness, own = 1.0, jax.random.fold_in(own_key, 6)
    for position, shards_of in pieces:
        steps = jnp.exp(jax.random.uniform(jax.random.fold_in(own, position), (shards_of,), jnp.float32, least / len(pieces), largest / len(pieces)))
        loudness = loudness * jnp.repeat(steps, dims[position] // shards_of).reshape([-1 if axis == position else 1 for axis in range(len(dims))])
    return loudness


def bell_draw(own_key, extent, scale, reach, shards=(), kind=jnp.bfloat16):
    drawn = jax.random.normal(own_key, extent, jnp.float32) * scale
    if len(shards) > 0:
        drawn = block_scale(own_key, extent, shards, -0.22, 0.18) * drawn
    return jnp.clip(drawn, min=-reach, max=reach).astype(kind)


def setup_inputs(seed: int = 0) -> dict:
    seeds = jax.random.split(jax.random.key(seed), 9)
    return {
        "half_ints": bell_draw(seeds[0], (AUX, NOCC, NBAS), 0.16, 1.0, ((0, 8), (1, 16))),
        "block_mask": touch_ends((jax.random.randint(seeds[1], (NBLK, NOCC), 0, 4) < 3).astype(jnp.int32), jax.random.fold_in(seeds[1], 1), 0, 1),
        "vir_coef": bell_draw(seeds[2], (NBAS, NVALL), NBAS ** -0.5, 0.1875),
        "domains": draw_domains(jax.random.fold_in(seeds[8], 71), 0),
        "vir_energy": jnp.clip(jax.random.uniform(seeds[4], (NVALL,), jnp.float32, 0.5, 3.0), 0.5, 3.0),
        "occ_energy": jnp.clip(jax.random.uniform(seeds[5], (NOCC,), jnp.float32, -3.0, -0.5), -3.0, -0.5),
        "pair_count": draw_pair_count(jax.random.fold_in(seeds[8], 71), 0),
        "pair_code": draw_pair_code(jax.random.fold_in(seeds[8], 71), 0),
    }


def reference(half_ints, block_mask, vir_coef, domains, vir_energy, occ_energy, pair_count, pair_code):
    row_mask = jnp.repeat(block_mask, BLK, axis=0).astype(jnp.bfloat16)

    def transform(orbital):
        columns = jnp.take(vir_coef, domains[orbital], axis=1)
        masked = half_ints[:, orbital, :] * row_mask[:, orbital][:, None]
        return jnp.dot(masked, columns, preferred_element_type=jnp.float32).astype(jnp.bfloat16)

    coupled = lax.map(transform, jnp.arange(NOCC, dtype=jnp.int32))
    span = PARTNERS * OCC_DEV

    def device_block(device):
        occ_pos = device // N_AUX
        aux_pos = device % N_AUX
        blocks = []
        dom_rows = []
        occ_rows = []
        for offset in range(PARTNERS):
            start = ((((occ_pos + offset) % N_OCC) * N_AUX + aux_pos) * OCC_DEV).astype(jnp.int32)
            blocks.append(lax.dynamic_slice_in_dim(coupled, start, OCC_DEV, 0))
            dom_rows.append(lax.dynamic_slice_in_dim(domains, start, OCC_DEV, 0))
            occ_rows.append(lax.dynamic_slice_in_dim(occ_energy, start, OCC_DEV, 0))
        partners = jnp.concatenate(blocks, axis=0)
        partner_vir = jnp.take(vir_energy, jnp.concatenate(dom_rows, axis=0))
        partner_occ = jnp.concatenate(occ_rows, axis=0)
        codes = pair_code[occ_pos, aux_pos]

        def pair_step(slot, gamma):
            code = codes[slot]
            own_slot = code // span
            partner_slot = code % span
            own_rows = partners[own_slot]
            partner_rows = partners[partner_slot]
            exchange = lax.dot_general(own_rows, partner_rows, (((0,), (0,)), ((), ())), preferred_element_type=jnp.float32)
            denom = partner_vir[own_slot][:, None] + partner_vir[partner_slot][None, :] - partner_occ[own_slot] - partner_occ[partner_slot]
            amplitude = (exchange / denom).astype(jnp.bfloat16)
            contrib = lax.dot_general(partner_rows, amplitude, (((1,), (1,)), ((), ())), preferred_element_type=jnp.float32)
            current = lax.dynamic_index_in_dim(gamma, own_slot, 0, keepdims=True)
            return lax.dynamic_update_index_in_dim(gamma, current + contrib[None], own_slot, 0)

        gamma = jnp.zeros((OCC_DEV, AUX, NVIR), jnp.float32)
        gamma = lax.fori_loop(0, pair_count[occ_pos, aux_pos], pair_step, gamma)
        return gamma.astype(jnp.bfloat16)

    result = lax.map(device_block, jnp.arange(N_OCC * N_AUX, dtype=jnp.int32))
    result = result.reshape(NOCC, AUX, NVIR)
    return jnp.transpose(result, (1, 0, 2))
```

```python
import functools

import jax
import jax.numpy as jnp
from jax import lax
from jax.experimental import pallas as pl
from jax.experimental.pallas import tpu as pltpu
from jax.sharding import PartitionSpec as P

BLK = 64
OCC = 4
K = 4
NQ = 8
MESH = pl.DeviceIdType.MESH


def gather_kernel(mask_ref, x_ref, coef_ref, dom_ref, out_ref, relay_ref,
                  xbuf, ybuf, cbuf, xsem, lsem, asend, arecv, bsend, brecv,
                  rsend, rrecv, isend, irecv, fsend, frecv, wsend, wrecv):
    q = lax.axis_index("aux")
    o = lax.axis_index("occ")
    core = o % 2
    x = (o // 2) % 4
    yl = o // 8
    rows = x_ref.shape[2]
    nvall = coef_ref.shape[1]
    nvir = out_ref.shape[2]

    def at(xx, yy, cc):
        return (q, (yy * 4 + xx % 4) * 2 + cc)

    def remote(src, dst, ssem, rsem, dev):
        return pltpu.make_async_remote_copy(
            src_ref=src, dst_ref=dst, send_sem=ssem, recv_sem=rsem,
            device_id=dev, device_id_type=MESH)

    def fetch(r):
        return pltpu.make_async_copy(x_ref.at[r], xbuf.at[r % 2], xsem.at[r % 2])

    prev_y = jnp.where(x == 0, 1 - yl, yl)
    relay_y = jnp.where(x >= 2, yl, 1 - yl)

    def exchange(r, d):
        to = (q + d) % NQ
        return remote(cbuf.at[r, to], out_ref.at[r, pl.ds(q * rows, rows)],
                      asend.at[r, d - 1], arecv.at[r, d - 1], (to, o))

    def keep(r):
        return pltpu.make_async_copy(
            cbuf.at[r, q], out_ref.at[r, pl.ds(q * rows, rows)], lsem.at[r])

    def onward(r):
        return remote(out_ref.at[r], out_ref.at[2 * OCC + r], bsend.at[r], brecv.at[r],
                      at(x + 3, prev_y, core))

    def detour(r):
        return remote(out_ref.at[r], relay_ref.at[r], rsend.at[r], rrecv.at[r],
                      at(0, 1 - yl, 1))

    def around(r):
        return remote(out_ref.at[r], relay_ref.at[r], rsend.at[r], rrecv.at[r],
                      at(x + 1, relay_y, 0))

    def to_core0(r):
        return remote(out_ref.at[r], out_ref.at[OCC + r], isend.at[r], irecv.at[r],
                      at(x, yl, 0))

    def share0(r):
        return remote(out_ref.at[2 * OCC + r], out_ref.at[OCC + r], fsend.at[r],
                      irecv.at[r], at(x, yl, 1))

    def share1(r):
        return remote(out_ref.at[2 * OCC + r], out_ref.at[3 * OCC + r], fsend.at[r],
                      frecv.at[r], at(x, yl, 0))

    def finish_around(r):
        return remote(relay_ref.at[r], out_ref.at[3 * OCC + r], wsend.at[r], frecv.at[r],
                      at(x + 1, yl, 1))

    def finish_detour(r):
        return remote(relay_ref.at[r], out_ref.at[2 * OCC + r], wsend.at[r], brecv.at[r],
                      at(3, yl, 1))

    def compute(r):
        fetch(r).wait()
        if r + 1 < OCC:
            fetch(r + 1).start()
        xs = xbuf.at[r % 2]

        def columns(n, _):
            c0 = pl.multiple_of(n * 256, 256)
            for h in range(2):
                half = NQ // 2
                part = xs[half * h:half * (h + 1)].reshape(half * rows, xs.shape[2])
                y = jnp.dot(part, coef_ref[:, pl.ds(c0, 256)],
                            preferred_element_type=jnp.float32)
                ybuf[half * h:half * (h + 1), :, pl.ds(c0, 256)] = y.astype(
                    jnp.bfloat16).reshape(half, rows, 256)
            return _

        lax.fori_loop(0, nvall // 256, columns, 0)

        def select(g, _):
            dom = dom_ref[r * NQ + g]
            def tile(n, acc):
                c0 = pl.multiple_of(n * 256, 256)
                ids = lax.broadcasted_iota(jnp.int32, (256, nvir), 0) + n * 256
                hot = jnp.where(ids == dom, 1.0, 0.0).astype(jnp.bfloat16)
                return acc + jnp.dot(ybuf[g, :, pl.ds(c0, 256)], hot,
                                     preferred_element_type=jnp.float32)
            acc = lax.fori_loop(0, nvall // 256, tile,
                                jnp.zeros((rows, nvir), jnp.float32))
            for b in range(rows // BLK):
                m = mask_ref[b, g * OCC + r].astype(jnp.float32)
                cbuf[r, g, b * BLK:(b + 1) * BLK, :] = (
                    acc[b * BLK:(b + 1) * BLK] * m).astype(jnp.bfloat16)
            return _

        lax.fori_loop(0, NQ, select, 0)

    fetch(0).start()
    first = jnp.logical_and(core == 1, x == 0)
    other = jnp.logical_not(first)
    for s in range(OCC + 2):
        if s < OCC:
            compute(s)
            keep(s).start()
            for d in range(1, NQ):
                exchange(s, d).start()
        if 1 <= s <= OCC:
            r = s - 1
            keep(r).wait()
            for d in range(1, NQ):
                exchange(r, d).wait_recv()

            @pl.when(core == 0)
            def _():
                around(r).start()

            @pl.when(first)
            def _():
                detour(r).start()

            @pl.when(other)
            def _():
                onward(r).start()

            @pl.when(core == 1)
            def _():
                to_core0(r).start()
        if s >= 2:
            r = s - 2

            @pl.when(core == 0)
            def _():
                around(r).wait_recv()
                finish_around(r).start()

            @pl.when(first)
            def _():
                detour(r).wait_recv()
                finish_detour(r).start()

            onward(r).wait_recv()

            @pl.when(core == 0)
            def _():
                share0(r).start()

            @pl.when(core == 1)
            def _():
                share1(r).start()

    for r in range(OCC):
        to_core0(r).wait_recv()
        share1(r).wait_recv()
        for d in range(1, NQ):
            exchange(r, d).wait_send()

        @pl.when(core == 0)
        def _():
            around(r).wait_send()
            finish_around(r).wait_send()
            share0(r).wait_send()

        @pl.when(first)
        def _():
            detour(r).wait_send()
            finish_detour(r).wait_send()

        @pl.when(other)
        def _():
            onward(r).wait_send()

        @pl.when(core == 1)
        def _():
            to_core0(r).wait_send()
            share1(r).wait_send()


def gather_partners(x, mask, coef, dom):
    _, _, rows, nbas = x.shape
    nvir = dom.shape[2]
    nvall = coef.shape[1]
    whole = jax.ShapeDtypeStruct((K * OCC, NQ * rows, nvir), jnp.bfloat16)
    relay = jax.ShapeDtypeStruct((OCC, NQ * rows, nvir), jnp.bfloat16)
    dma = pltpu.SemaphoreType.DMA
    return pl.pallas_call(
        gather_kernel,
        out_shape=(whole, relay),
        in_specs=[
            pl.BlockSpec(memory_space=pltpu.SMEM),
            pl.BlockSpec(memory_space=pl.ANY),
            pl.BlockSpec(memory_space=pltpu.VMEM),
            pl.BlockSpec(memory_space=pltpu.VMEM),
        ],
        out_specs=(pl.BlockSpec(memory_space=pl.ANY), pl.BlockSpec(memory_space=pl.ANY)),
        scratch_shapes=[
            pltpu.VMEM((2, NQ, rows, nbas), jnp.bfloat16),
            pltpu.VMEM((NQ, rows, nvall), jnp.bfloat16),
            pltpu.VMEM((OCC, NQ, rows, nvir), jnp.bfloat16),
            dma((2,)), dma((OCC,)),
            dma((OCC, NQ - 1)), dma((OCC, NQ - 1)),
            dma((OCC,)), dma((OCC,)),
            dma((OCC,)), dma((OCC,)),
            dma((OCC,)), dma((OCC,)),
            dma((OCC,)), dma((OCC,)),
            dma((OCC,)), dma((OCC,)),
        ],
        compiler_params=pltpu.CompilerParams(has_side_effects=True, vmem_limit_bytes=40 << 20),
        name="transform_exchange",
    )(mask, x, coef, dom)[0]


def pair_kernel(count_ref, code_ref, occ_ref, ints_ref, dom_ref, vir_ref, out_ref,
                own, partner, total, energy, order, osem, psem, dsem):
    n_aux = ints_ref.shape[1]
    nvir = ints_ref.shape[2]
    count = count_ref[0, 0]
    span = K * OCC

    def load_own(t):
        return pltpu.make_async_copy(ints_ref.at[t], own.at[0], osem.at[0])

    def load_partner(n):
        ku = code_ref[0, 0, order[n]] % span
        return pltpu.make_async_copy(ints_ref.at[ku], partner.at[n % 2], psem.at[n % 2])

    low = dom_ref[...] % 128
    high = dom_ref[...] // 128
    for row in range(0, span, 8):
        for c in range(0, nvir, 128):
            lo = low[row:row + 8, c:c + 128]
            hi = high[row:row + 8, c:c + 128]
            acc = jnp.zeros((8, 128), jnp.float32)
            for b in range(vir_ref.shape[0]):
                table = jnp.broadcast_to(vir_ref[b:b + 1, :], (8, 128))
                picked = jnp.take_along_axis(table, lo, axis=1)
                acc = jnp.where(hi == b, picked, acc)
            energy[row:row + 8, c:c + 128] = acc

    def per_own(t, start):
        def scan(s, n):
            hit = jnp.logical_and(s < count, code_ref[0, 0, s] // span == t)

            @pl.when(hit)
            def _():
                order[n] = s
            return n + hit.astype(jnp.int32)

        n_pairs = lax.fori_loop(0, code_ref.shape[2], scan, 0)
        load_own(t).start()

        @pl.when(n_pairs > 0)
        def _():
            load_partner(0).start()

        total[...] = jnp.zeros_like(total)
        load_own(t).wait()
        own[1] = own[0]
        occ_i = occ_ref[t]
        column = jnp.transpose(jnp.broadcast_to(energy[pl.ds(t, 1), :], (128, nvir)))

        def pair(n, carry):
            load_partner(n).wait()

            @pl.when(n + 1 < n_pairs)
            def _():
                load_partner(n + 1).start()

            ku = code_ref[0, 0, order[n]] % span
            held = partner.at[n % 2]
            ex = lax.dot_general(own[0], held[...], (((0,), (0,)), ((), ())),
                                 preferred_element_type=jnp.float32)
            denom = (jnp.concatenate([column] * (nvir // 128), axis=1)
                     + energy[pl.ds(ku, 1), :] - occ_i - occ_ref[ku])
            amp = (ex / denom).astype(jnp.bfloat16)
            total[...] += lax.dot_general(held[...], amp, (((1,), (1,)), ((), ())),
                                          preferred_element_type=jnp.float32)
            return carry

        lax.fori_loop(0, n_pairs, pair, 0)

        @pl.when(t > 0)
        def _():
            pltpu.make_async_copy(own.at[1], out_ref.at[0], dsem).wait()
        own[1] = total[...].astype(jnp.bfloat16)
        pltpu.make_async_copy(own.at[1], out_ref.at[t], dsem).start()
        return start

    lax.fori_loop(0, OCC, per_own, 0)
    pltpu.make_async_copy(own.at[1], out_ref.at[0], dsem).wait()


def pair_density(count, codes, occ, ints, dom, vir):
    span, n_aux, nvir = ints.shape
    smem = pl.BlockSpec(memory_space=pltpu.SMEM)
    vmem = pl.BlockSpec(memory_space=pltpu.VMEM)
    dma = pltpu.SemaphoreType.DMA
    return pl.pallas_call(
        pair_kernel,
        out_shape=jax.ShapeDtypeStruct((OCC, n_aux, nvir), jnp.bfloat16),
        in_specs=[smem, smem, smem, pl.BlockSpec(memory_space=pl.ANY), vmem, vmem],
        out_specs=pl.BlockSpec(memory_space=pl.ANY),
        scratch_shapes=[
            pltpu.VMEM((2, n_aux, nvir), jnp.bfloat16),
            pltpu.VMEM((2, n_aux, nvir), jnp.bfloat16),
            pltpu.VMEM((n_aux, nvir), jnp.float32),
            pltpu.VMEM((span, nvir), jnp.float32),
            pltpu.SMEM((codes.shape[2],), jnp.int32),
            dma((1,)), dma((2,)), dma(()),
        ],
        compiler_params=pltpu.CompilerParams(vmem_limit_bytes=40 << 20),
        name="pair_density",
    )(count, codes, occ, ints, dom, vir)


def body(half_ints, block_mask, vir_coef, domains, vir_energy, occ_energy, pair_count, pair_code):
    aux_count = lax.axis_size("aux")
    occ_count = lax.axis_size("occ")
    aux_pos = lax.axis_index("aux")
    occ_pos = lax.axis_index("occ")
    rows, local, nbas = half_ints.shape
    nvir = domains.shape[1]
    x = half_ints.reshape(rows, NQ, OCC, nbas).transpose(2, 1, 0, 3)
    own_domains = lax.dynamic_slice_in_dim(domains, occ_pos * local, local, 0)
    dom = own_domains.reshape(NQ, OCC, nvir).transpose(1, 0, 2).reshape(local, 1, nvir)
    ints = gather_partners(x, block_mask, vir_coef, dom)
    dom_rows = []
    occ_rows = []
    for offset in range(K):
        start = ((occ_pos + offset) % occ_count * aux_count + aux_pos) * OCC
        dom_rows.append(lax.dynamic_slice_in_dim(domains, start, OCC, 0))
        occ_rows.append(lax.dynamic_slice_in_dim(occ_energy, start, OCC, 0))
    density = pair_density(
        pair_count, pair_code, jnp.concatenate(occ_rows), ints,
        jnp.concatenate(dom_rows, axis=0), vir_energy.reshape(-1, 128))
    split = density.reshape(OCC, NQ, rows, nvir)
    back = lax.all_to_all(split, "aux", split_axis=1, concat_axis=1, tiled=True)
    return back.transpose(2, 1, 0, 3).reshape(rows, local, nvir)


def solution(mesh):
    placed = (
        P("aux", "occ", None),
        P("aux", "occ"),
        P(),
        P(),
        P(),
        P(),
        P("occ", "aux"),
        P("occ", "aux", None),
    )
    return jax.shard_map(
        body, mesh=mesh, in_specs=placed, out_specs=P("aux", "occ", None), check_vma=False
    )
```

```python
import functools

import jax
import jax.numpy as jnp
from jax import lax
from jax.experimental import pallas as pl
from jax.experimental.pallas import tpu as pltpu
from jax.sharding import PartitionSpec as P

BLK = 64
OCC = 4
K = 4
NQ = 8
MESH = pl.DeviceIdType.MESH


def peer(q, d):
    return (q // 4 + d % 2) % 2 * 4 + (q + d // 2) % 4


def meet(devices):
    barrier = pltpu.get_barrier_semaphore()
    for device in devices:
        pl.semaphore_signal(barrier, inc=1, device_id=device, device_id_type=MESH)
    pl.semaphore_wait(barrier, len(devices))


def gather_kernel(mask_ref, x_ref, coef_ref, dom_ref, out_ref, relay_ref,
                  raw, xall, ybuf, cbuf, ids, doms, dsem, xsem, lsem, asend, arecv, bsend, brecv,
                  rsend, rrecv, isend, irecv, fsend, frecv, wsend):
    q = lax.axis_index("aux")
    o = lax.axis_index("occ")
    core = o % 2
    x = (o // 2) % 4
    yl = o // 8
    rows = x_ref.shape[0]
    nbas = x_ref.shape[2]
    nvall = coef_ref.shape[1]
    nvir = out_ref.shape[-1]
    tile = 256
    prev_y = jnp.where(x == 0, 1 - yl, yl)
    relay_y = jnp.where(x >= 2, yl, 1 - yl)
    first = jnp.logical_and(core == 1, x == 0)
    other = jnp.logical_not(first)

    def at(xx, yy, cc):
        return (q, (yy * 4 + xx % 4) * 2 + cc)

    def remote(src, dst, ssem, rsem, dev):
        return pltpu.make_async_remote_copy(
            src_ref=src, dst_ref=dst, send_sem=ssem, recv_sem=rsem,
            device_id=dev, device_id_type=MESH)

    def fetch(g):
        return pltpu.make_async_copy(x_ref.at[pl.ds(g * 16, 16)], raw.at[g], xsem.at[g])

    def exchange(r, h, d):
        to = peer(q, d)
        return remote(cbuf.at[r, h, to], out_ref.at[r, h, q],
                      asend.at[r, h, d - 1], arecv.at[r, h, d - 1], (to, o))

    def keep(r, h):
        return pltpu.make_async_copy(cbuf.at[r, h, q], out_ref.at[r, h, q], lsem.at[r, h])

    def onward(r, h):
        return remote(out_ref.at[r, h], out_ref.at[2 * OCC + r, h], bsend.at[r, h],
                      brecv.at[r, h], at(x + 3, prev_y, core))

    def detour(r, h):
        return remote(out_ref.at[r, h], relay_ref.at[r, h], rsend.at[r, h], rrecv.at[r, h],
                      at(0, 1 - yl, 1))

    def around(r, h):
        return remote(out_ref.at[r, h], relay_ref.at[r, h], rsend.at[r, h], rrecv.at[r, h],
                      at(x + 1, relay_y, 0))

    def to_core0(r, h):
        return remote(out_ref.at[r, h], out_ref.at[OCC + r, h], isend.at[r, h],
                      irecv.at[r, h], at(x, yl, 0))

    def share0(r, h):
        return remote(out_ref.at[2 * OCC + r, h], out_ref.at[OCC + r, h], fsend.at[r, h],
                      irecv.at[r, h], at(x, yl, 1))

    def share1(r, h):
        return remote(out_ref.at[2 * OCC + r, h], out_ref.at[3 * OCC + r, h],
                      fsend.at[r, h], frecv.at[r, h], at(x, yl, 0))

    def finish_around(r, h):
        return remote(relay_ref.at[r, h], out_ref.at[3 * OCC + r, h], wsend.at[r, h],
                      frecv.at[r, h], at(x + 1, yl, 1))

    def finish_detour(r, h):
        return remote(relay_ref.at[r, h], out_ref.at[2 * OCC + r, h], wsend.at[r, h],
                      brecv.at[r, h], at(3, yl, 1))

    def regroup():
        size = 8 * NQ * OCC
        row = lax.broadcasted_iota(jnp.int32, (size, size), 0)
        col = lax.broadcasted_iota(jnp.int32, (size, size), 1)
        source = (row % 8) * (NQ * OCC) + ((row // 8) % NQ) * OCC + row // (8 * NQ)
        moved = jnp.where(col == source, 1.0, 0.0).astype(jnp.bfloat16)
        ids[...] = lax.broadcasted_iota(jnp.int32, ids.shape, 0).astype(
            jnp.float32).astype(jnp.bfloat16)

        def group(g, carry):
            fetch(g).wait()
            halves = []
            for half in range(2):
                part = raw[g, 8 * half:8 * half + 8].reshape(size, nbas)
                halves.append(jnp.dot(moved, part, preferred_element_type=jnp.float32)
                              .reshape(NQ * OCC, 8, nbas))
            xall[:, pl.ds(pl.multiple_of(g * 16, 16), 16), :] = jnp.concatenate(
                halves, axis=1).astype(jnp.bfloat16)
            return carry

        lax.fori_loop(0, rows // 16, group, 0)

    def transform(r):
        def columns(n, carry):
            c0 = pl.multiple_of(n * tile, tile)
            for h in range(2):
                half = NQ // 2
                g0 = r * NQ + half * h
                part = xall[g0:g0 + half].reshape(half * rows, nbas)
                y = jnp.dot(part, coef_ref[:, pl.ds(c0, tile)],
                            preferred_element_type=jnp.float32)
                ybuf[half * h:half * (h + 1), :, pl.ds(c0, tile)] = y.astype(
                    jnp.bfloat16).reshape(half, rows, tile)
            return carry

        lax.fori_loop(0, nvall // tile, columns, 0)

    def select(r):
        def orbital(g, carry):
            dom = doms[pl.ds(g * OCC + r, 1), :]
            hot = []
            for n in range(nvall // tile):
                near = dom - n * tile
                inside = jnp.logical_and(near >= 0, near < tile)
                near = jnp.where(inside, near, -1).astype(jnp.float32).astype(jnp.bfloat16)
                hot.append(jnp.where(ids[...] == near, jnp.bfloat16(1), jnp.bfloat16(0)))
            acc = jnp.dot(ybuf[g], jnp.concatenate(hot, axis=0),
                          preferred_element_type=jnp.float32)
            for b in range(rows // BLK):
                m = mask_ref[b, g * OCC + r].astype(jnp.float32)
                cbuf[r, b, g] = (acc[b * BLK:(b + 1) * BLK] * m).astype(jnp.bfloat16)
            return carry

        lax.fori_loop(0, NQ, orbital, 0)
        for h in range(2):
            for d in range(1, NQ):
                exchange(r, h, d).start()
            keep(r, h).start()

    def send_on(r, h):
        keep(r, h).wait()
        for d in range(1, NQ):
            exchange(r, h, d).wait_recv()

        @pl.when(core == 0)
        def _():
            around(r, h).start()

        @pl.when(first)
        def _():
            detour(r, h).start()

        @pl.when(other)
        def _():
            onward(r, h).start()

        @pl.when(core == 1)
        def _():
            to_core0(r, h).start()

    def forward(r, h):
        @pl.when(core == 0)
        def _():
            around(r, h).wait_recv()
            finish_around(r, h).start()

        @pl.when(first)
        def _():
            detour(r, h).wait_recv()
            finish_detour(r, h).start()

        onward(r, h).wait_recv()

        @pl.when(core == 0)
        def _():
            share0(r, h).start()

        @pl.when(core == 1)
        def _():
            share1(r, h).start()

    mine = pltpu.make_async_copy(
        dom_ref.at[pl.ds(pl.multiple_of(o * doms.shape[0], 8), doms.shape[0])], doms, dsem)
    mine.start()
    for g in range(rows // 16):
        fetch(g).start()
    regroup()
    mine.wait()
    n_occ = lax.axis_size("occ")
    meet([(peer(q, d), o) for d in range(1, NQ)]
         + [(q, (o + d) % n_occ) for d in range(1, n_occ)])
    for s in range(OCC + 2):
        for h in range(2):
            if s < OCC and h == 0:
                transform(s)
            if s < OCC and h == 1:
                select(s)
            if 1 <= s <= OCC:
                send_on(s - 1, h)
            if s >= 2:
                forward(s - 2, h)

    for r in range(OCC):
        for h in range(2):
            to_core0(r, h).wait_recv()
            share1(r, h).wait_recv()
            for d in range(1, NQ):
                exchange(r, h, d).wait_send()

            @pl.when(core == 0)
            def _():
                around(r, h).wait_send()
                finish_around(r, h).wait_send()
                share0(r, h).wait_send()

            @pl.when(first)
            def _():
                detour(r, h).wait_send()
                finish_detour(r, h).wait_send()

            @pl.when(other)
            def _():
                onward(r, h).wait_send()

            @pl.when(core == 1)
            def _():
                to_core0(r, h).wait_send()
                share1(r, h).wait_send()


def gather_partners(x, mask, coef, dom):
    rows, local, nbas = x.shape
    nvir = dom.shape[1]
    nvall = coef.shape[1]
    halves = rows // BLK
    whole = jax.ShapeDtypeStruct((K * OCC, halves, NQ, BLK, nvir), jnp.bfloat16)
    relay = jax.ShapeDtypeStruct((OCC, halves, NQ, BLK, nvir), jnp.bfloat16)
    dma = pltpu.SemaphoreType.DMA
    return pl.pallas_call(
        gather_kernel,
        out_shape=(whole, relay),
        in_specs=[
            pl.BlockSpec(memory_space=pltpu.SMEM),
            pl.BlockSpec(memory_space=pl.ANY),
            pl.BlockSpec(memory_space=pltpu.VMEM),
            pl.BlockSpec(memory_space=pl.ANY),
        ],
        out_specs=(pl.BlockSpec(memory_space=pl.ANY), pl.BlockSpec(memory_space=pl.ANY)),
        scratch_shapes=[
            pltpu.VMEM((rows // 16, 16, local, nbas), jnp.bfloat16),
            pltpu.VMEM((local, rows, nbas), jnp.bfloat16),
            pltpu.VMEM((NQ, rows, nvall), jnp.bfloat16),
            pltpu.VMEM((OCC, halves, NQ, BLK, nvir), jnp.bfloat16),
            pltpu.VMEM((256, nvir), jnp.bfloat16),
            pltpu.VMEM((local, nvir), jnp.int32), dma(()),
            dma((rows // 16,)), dma((OCC, halves)),
            dma((OCC, halves, NQ - 1)), dma((OCC, halves, NQ - 1)),
        ] + [dma((OCC, halves))] * 9,
        compiler_params=pltpu.CompilerParams(collective_id=0, has_side_effects=True,
                                             vmem_limit_bytes=48 << 20),
        name="transform_exchange",
    )(mask, x, coef, dom)[0]


def pair_kernel(slot_ref, occ_ref, ints_ref, dom_ref, vir_ref, out_ref,
                parts, own, column, energy, doms, amp, run, snap, outbox, dsem, psem, lsem, ssem, rsem):
    q = lax.axis_index("aux")
    o = lax.axis_index("occ")
    span, n_aux, nvir = parts.shape
    pieces = outbox.shape[0]
    wide = nvir // pieces
    slots = slot_ref.shape[1]

    n_occ = lax.axis_size("occ")
    low_half = (q % 2) * OCC

    def landing(c):
        return out_ref.at[q, :, :, :, pl.ds(c * wide, wide)]

    def row_of(ku):
        return (ku // OCC) * 8 + low_half + ku % OCC

    def occupied(ku):
        return occ_ref[((o + ku // OCC) % n_occ * NQ + q) * OCC + ku % OCC]

    def names(k):
        first = ((o + k) % n_occ * NQ + q) // 2 * 8
        return pltpu.make_async_copy(dom_ref.at[pl.ds(pl.multiple_of(first, 8), 8)],
                                     doms.at[k], dsem.at[k])

    def load(j):
        return pltpu.make_async_copy(ints_ref.at[j], parts.at[j], psem.at[j])

    def send(c, d):
        to = peer(q, d)
        return pltpu.make_async_remote_copy(
            src_ref=outbox.at[c, to], dst_ref=landing(c), send_sem=ssem.at[c, d - 1],
            recv_sem=rsem.at[c, d - 1], device_id=(to, o), device_id_type=MESH)

    def keep(c):
        return pltpu.make_async_copy(outbox.at[c, q], landing(c), lsem.at[c])

    for k in range(K):
        names(k).start()
    for j in range(span):
        load(j).start()
    meet([(peer(q, d), o) for d in range(1, NQ)])
    for k in range(K):
        names(k).wait()
        low = doms[k] % 128
        high = doms[k] // 128
        for c in range(0, nvir, 128):
            acc = jnp.zeros((8, 128), jnp.float32)
            for b in range(vir_ref.shape[0]):
                table = jnp.broadcast_to(vir_ref[b:b + 1, :], (8, 128))
                picked = jnp.take_along_axis(table, low[:, c:c + 128], axis=1)
                acc = jnp.where(high[:, c:c + 128] == b, picked, acc)
            for i in range(8):
                energy[k * 8 + i, :, c:c + 128] = acc[i:i + 1]
    for t in range(OCC):
        column[t] = jnp.transpose(jnp.broadcast_to(energy[row_of(t)], (128, nvir)))
    for t in range(OCC):
        load(t).wait()

    def flip(t, carry):
        for c in range(pieces):
            own[t, c] = jnp.transpose(parts[t, :, c * wide:(c + 1) * wide])
        return carry

    lax.fori_loop(0, OCC, flip, 0)
    for j in range(OCC, span):
        load(j).wait()

    for c in range(pieces):
        def amplitude(n):
            t = slot_ref[0, n]
            ku = slot_ref[1, n]
            ex = jnp.dot(own[t, c], parts[ku], preferred_element_type=jnp.float32)
            mine = column[t, c * wide:(c + 1) * wide, :]
            denom = (jnp.concatenate([mine] * (nvir // 128), axis=1) + energy[row_of(ku)]
                     - occupied(t) - occupied(ku))
            live = slot_ref[2, n].astype(jnp.float32)
            amp[n % 2] = (ex / denom * live).astype(jnp.bfloat16)

        def contract(n):
            add = lax.dot_general(parts[slot_ref[1, n]], amp[n % 2], (((1,), (1,)), ((), ())),
                                  preferred_element_type=jnp.float32)
            same = slot_ref[3, n].astype(jnp.float32)
            total = run[...] * same + add
            run[...] = total
            snap[n] = total.astype(jnp.bfloat16)

        run[...] = jnp.zeros_like(run)
        amplitude(0)

        def step(n, carry):
            contract(n - 1)
            amplitude(n)
            return carry

        lax.fori_loop(1, slots, step, 0)
        contract(slots - 1)
        for t in range(OCC):
            some = slot_ref[5, t].astype(jnp.float32).astype(jnp.bfloat16)
            last = snap[slot_ref[4, t]] * some
            for h in range(n_aux // (NQ * BLK)):
                for p in range(NQ):
                    r0 = (h * NQ + p) * BLK
                    outbox[c, p, t, h] = last[r0:r0 + BLK]
        for d in range(1, NQ):
            send(c, d).start()
        keep(c).start()
    for c in range(pieces):
        keep(c).wait()
        for d in range(1, NQ):
            send(c, d).wait()


def pair_density(slots, occ, ints, dom, vir, pieces):
    span, n_aux, nvir = ints.shape
    wide = nvir // pieces
    halves = n_aux // (NQ * BLK)
    smem = pl.BlockSpec(memory_space=pltpu.SMEM)
    vmem = pl.BlockSpec(memory_space=pltpu.VMEM)
    dma = pltpu.SemaphoreType.DMA
    box = (pieces, NQ, OCC, halves, BLK, wide)
    return pl.pallas_call(
        pair_kernel,
        out_shape=jax.ShapeDtypeStruct((NQ, OCC, halves, BLK, nvir), jnp.bfloat16),
        in_specs=[smem, smem, pl.BlockSpec(memory_space=pl.ANY),
                  pl.BlockSpec(memory_space=pl.ANY), vmem],
        out_specs=pl.BlockSpec(memory_space=pl.ANY),
        scratch_shapes=[
            pltpu.VMEM((span, n_aux, nvir), jnp.bfloat16),
            pltpu.VMEM((OCC, pieces, wide, n_aux), jnp.bfloat16),
            pltpu.VMEM((OCC, nvir, 128), jnp.float32),
            pltpu.VMEM((2 * span, 1, nvir), jnp.float32),
            pltpu.VMEM((K, 8, nvir), jnp.int32),
            pltpu.VMEM((2, wide, nvir), jnp.bfloat16),
            pltpu.VMEM((n_aux, wide), jnp.float32),
            pltpu.VMEM((slots.shape[1], n_aux, wide), jnp.bfloat16),
            pltpu.VMEM(box, jnp.bfloat16),
            dma((K,)), dma((span,)), dma((pieces,)), dma((pieces, NQ - 1)), dma((pieces, NQ - 1)),
        ],
        compiler_params=pltpu.CompilerParams(collective_id=1, has_side_effects=True,
                                             vmem_limit_bytes=48 << 20),
        name="pair_density",
    )(slots, occ, ints, dom, vir)


def slot_kernel(count_ref, code_ref, out_ref):
    span = K * OCC
    cap = code_ref.shape[2]
    count = count_ref[0, 0]

    def clear(n, carry):
        out_ref[0, n] = 0
        out_ref[1, n] = 0
        out_ref[2, n] = 0
        out_ref[3, n] = 0
        return carry

    lax.fori_loop(0, cap, clear, 0)
    at = jnp.int32(0)
    for t in range(OCC):
        begin = at

        def scan(s, n):
            code = code_ref[0, 0, s]
            hit = code // span == t

            @pl.when(hit)
            def _():
                out_ref[0, n] = t
                out_ref[1, n] = code % span
                out_ref[2, n] = 1
                out_ref[3, n] = (n > begin).astype(jnp.int32)
            return n + hit.astype(jnp.int32)

        at = lax.fori_loop(0, count, scan, at)
        out_ref[4, t] = jnp.maximum(at - 1, 0)
        out_ref[5, t] = (at > begin).astype(jnp.int32)


def slot_table(count, codes):
    smem = pl.BlockSpec(memory_space=pltpu.SMEM)
    return pl.pallas_call(
        slot_kernel,
        out_shape=jax.ShapeDtypeStruct((6, codes.shape[2]), jnp.int32),
        in_specs=[smem, smem],
        out_specs=smem,
        name="slot_table",
    )(count, codes)


def body(half_ints, block_mask, vir_coef, domains, vir_energy, occ_energy, pair_count, pair_code):
    rows, local, _ = half_ints.shape
    nvir = domains.shape[1]
    ints = gather_partners(half_ints, block_mask, vir_coef, domains)
    density = pair_density(
        slot_table(pair_count, pair_code), occ_energy,
        ints.reshape(K * OCC, NQ * rows, nvir), domains, vir_energy.reshape(-1, 128), 2)
    return density.transpose(2, 3, 0, 1, 4).reshape(rows, local, nvir)


def solution(mesh):
    placed = (
        P("aux", "occ", None),
        P("aux", "occ"),
        P(),
        P(),
        P(),
        P(),
        P("occ", "aux"),
        P("occ", "aux", None),
    )
    return jax.shard_map(
        body, mesh=mesh, in_specs=placed, out_specs=P("aux", "occ", None), check_vma=False
    )
```

```python
import functools

import jax
import jax.numpy as jnp
from jax import lax
from jax.experimental import pallas as pl
from jax.experimental.pallas import tpu as pltpu
from jax.sharding import PartitionSpec as P

BLK = 64
OCC = 4
K = 4
NQ = 8
MESH = pl.DeviceIdType.MESH


def timeline():
    steps = []
    for s in range(OCC + 2):
        if s < OCC:
            steps.append(("transform", s, 0))
        if 1 <= s <= OCC:
            steps.append(("send", s - 1, 0))
        if s >= 2:
            steps += [("relay", s - 2, 1), ("share", s - 2, 0)]
        if s < OCC:
            steps.append(("select", s, 0))
        if 1 <= s <= OCC:
            steps += [("relay", s - 1, 0), ("send", s - 1, 1)]
        if s == OCC:
            steps.append(("prepare", 0, 0))
        if s >= 2:
            steps.append(("share", s - 2, 1))
    return steps


ORDER = timeline()


def peer(q, d):
    return (q // 4 + d % 2) % 2 * 4 + (q + d // 2) % 4


def meet(devices):
    barrier = pltpu.get_barrier_semaphore()
    for device in devices:
        pl.semaphore_signal(barrier, inc=1, device_id=device, device_id_type=MESH)
    pl.semaphore_wait(barrier, len(devices))


def fused_kernel(slot_ref, mask_ref, occ_ref, x_ref, coef_ref, dom_ref, vir_ref, out_ref,
                 relay_ref, parts, cbuf, outbox, own, column, energy, ids, doms, near,
                 dsem, xsem, lsem, asend, arecv, bsend, brecv, rsend, rrecv, isend, irecv,
                 fsend, frecv, wsend, nsem, ksem, ssem, dens_sem):
    q = lax.axis_index("aux")
    o = lax.axis_index("occ")
    core = o % 2
    x = (o // 2) % 4
    yl = o // 8
    rows = x_ref.shape[0]
    nbas = x_ref.shape[2]
    nvall = coef_ref.shape[1]
    nvir = parts.shape[-1]
    span = parts.shape[0]
    n_aux = rows * NQ
    n_occ = lax.axis_size("occ")
    low_half = (q % 2) * OCC
    tile = 256
    prev_y = jnp.where(x == 0, 1 - yl, yl)
    relay_y = jnp.where(x >= 2, yl, 1 - yl)
    first = jnp.logical_and(core == 1, x == 0)
    other = jnp.logical_not(first)

    def at(xx, yy, cc):
        return (q, (yy * 4 + xx % 4) * 2 + cc)

    def remote(src, dst, ssem, rsem, dev):
        return pltpu.make_async_remote_copy(
            src_ref=src, dst_ref=dst, send_sem=ssem, recv_sem=rsem,
            device_id=dev, device_id_type=MESH)

    def fetch(g, raw):
        return pltpu.make_async_copy(x_ref.at[pl.ds(g * 16, 16)], raw.at[g], xsem.at[g])

    def exchange(r, h, d):
        to = peer(q, d)
        return remote(cbuf.at[r, h, to], parts.at[r, h, q],
                      asend.at[r, h, d - 1], arecv.at[r, h, d - 1], (to, o))

    def keep(r, h):
        return pltpu.make_async_copy(cbuf.at[r, h, q], parts.at[r, h, q], lsem.at[r, h])

    def onward(r, h):
        return remote(parts.at[r, h], parts.at[2 * OCC + r, h], bsend.at[r, h],
                      brecv.at[r, h], at(x + 3, prev_y, core))

    def detour(r, h):
        return remote(parts.at[r, h], relay_ref.at[r, h], rsend.at[r, h], rrecv.at[r, h],
                      at(0, 1 - yl, 1))

    def around(r, h):
        return remote(parts.at[r, h], relay_ref.at[r, h], rsend.at[r, h], rrecv.at[r, h],
                      at(x + 1, relay_y, 0))

    def to_core0(r, h):
        return remote(parts.at[r, h], parts.at[OCC + r, h], isend.at[r, h],
                      irecv.at[r, h], at(x, yl, 0))

    def share0(r, h):
        return remote(parts.at[2 * OCC + r, h], parts.at[OCC + r, h], fsend.at[r, h],
                      irecv.at[r, h], at(x, yl, 1))

    def share1(r, h):
        return remote(parts.at[2 * OCC + r, h], parts.at[3 * OCC + r, h],
                      fsend.at[r, h], frecv.at[r, h], at(x, yl, 0))

    def finish_around(r, h):
        return remote(relay_ref.at[r, h], parts.at[3 * OCC + r, h], wsend.at[r, h],
                      frecv.at[r, h], at(x + 1, yl, 1))

    def finish_detour(r, h):
        return remote(relay_ref.at[r, h], parts.at[2 * OCC + r, h], wsend.at[r, h],
                      brecv.at[r, h], at(3, yl, 1))

    def regroup(raw, xall):
        size = 8 * NQ * OCC
        row = lax.broadcasted_iota(jnp.int32, (size, size), 0)
        col = lax.broadcasted_iota(jnp.int32, (size, size), 1)
        source = (row % 8) * (NQ * OCC) + ((row // 8) % NQ) * OCC + row // (8 * NQ)
        moved = jnp.where(col == source, 1.0, 0.0).astype(jnp.bfloat16)
        ids[...] = lax.broadcasted_iota(jnp.int32, ids.shape, 0).astype(
            jnp.float32).astype(jnp.bfloat16)

        def group(g, carry):
            fetch(g, raw).wait()
            halves = []
            for half in range(2):
                part = raw[g, 8 * half:8 * half + 8].reshape(size, nbas)
                halves.append(jnp.dot(moved, part, preferred_element_type=jnp.float32)
                              .reshape(NQ * OCC, 8, nbas))
            xall[:, pl.ds(pl.multiple_of(g * 16, 16), 16), :] = jnp.concatenate(
                halves, axis=1).astype(jnp.bfloat16)
            return carry

        lax.fori_loop(0, rows // 16, group, 0)

    def transform(r, xall, ybuf):
        def columns(n, carry):
            c0 = pl.multiple_of(n * tile, tile)
            for h in range(2):
                half = NQ // 2
                g0 = r * NQ + half * h
                part = xall[g0:g0 + half].reshape(half * rows, nbas)
                y = jnp.dot(part, coef_ref[:, pl.ds(c0, tile)],
                            preferred_element_type=jnp.float32)
                ybuf[half * h:half * (h + 1), :, pl.ds(c0, tile)] = y.astype(
                    jnp.bfloat16).reshape(half, rows, tile)
            return carry

        lax.fori_loop(0, nvall // tile, columns, 0)

    def select(r, ybuf):
        def orbital(g, carry):
            dom = doms[pl.ds(g * OCC + r, 1), :]
            hot = []
            for n in range(nvall // tile):
                near = dom - n * tile
                inside = jnp.logical_and(near >= 0, near < tile)
                near = jnp.where(inside, near, -1).astype(jnp.float32).astype(jnp.bfloat16)
                hot.append(jnp.where(ids[...] == near, jnp.bfloat16(1), jnp.bfloat16(0)))
            acc = jnp.dot(ybuf[g], jnp.concatenate(hot, axis=0),
                          preferred_element_type=jnp.float32)
            for b in range(rows // BLK):
                m = mask_ref[b, g * OCC + r].astype(jnp.float32)
                cbuf[r, b, g] = (acc[b * BLK:(b + 1) * BLK] * m).astype(jnp.bfloat16)
            return carry

        lax.fori_loop(0, NQ, orbital, 0)
        for h in range(2):
            for d in range(1, NQ):
                exchange(r, h, d).start()
            keep(r, h).start()

    def send_on(r, h):
        keep(r, h).wait()
        for d in range(1, NQ):
            exchange(r, h, d).wait_recv()

        @pl.when(core == 0)
        def _():
            around(r, h).start()

        @pl.when(first)
        def _():
            detour(r, h).start()

        @pl.when(other)
        def _():
            onward(r, h).start()

        @pl.when(core == 1)
        def _():
            to_core0(r, h).start()

    def relay(r, h):
        @pl.when(core == 0)
        def _():
            around(r, h).wait_recv()
            finish_around(r, h).start()

        @pl.when(first)
        def _():
            detour(r, h).wait_recv()
            finish_detour(r, h).start()

    def share(r, h):
        onward(r, h).wait_recv()

        @pl.when(core == 0)
        def _():
            share0(r, h).start()

        @pl.when(core == 1)
        def _():
            share1(r, h).start()

    pieces = outbox.shape[0]
    wide = nvir // pieces
    slots = slot_ref.shape[1]

    def landing(c):
        return out_ref.at[q, :, :, :, pl.ds(c * wide, wide)]

    def row_of(ku):
        return (ku // OCC) * 8 + low_half + ku % OCC

    def occupied(ku):
        return occ_ref[((o + ku // OCC) % n_occ * NQ + q) * OCC + ku % OCC]

    def names(k):
        first = ((o + k) % n_occ * NQ + q) // 2 * 8
        return pltpu.make_async_copy(dom_ref.at[pl.ds(pl.multiple_of(first, 8), 8)],
                                     near.at[k], nsem.at[k])

    def send(c, d):
        to = peer(q, d)
        return pltpu.make_async_remote_copy(
            src_ref=outbox.at[c, to], dst_ref=landing(c), send_sem=ssem.at[c, d - 1],
            recv_sem=dens_sem.at[c, d - 1], device_id=(to, o), device_id_type=MESH)

    def keep_box(c):
        return pltpu.make_async_copy(outbox.at[c, q], landing(c), ksem.at[c])

    def prepare():
        for k in range(K):
            names(k).wait()
            low = near[k] % 128
            high = near[k] // 128
            for c in range(0, nvir, 128):
                acc = jnp.zeros((8, 128), jnp.float32)
                for b in range(vir_ref.shape[0]):
                    table = jnp.broadcast_to(vir_ref[b:b + 1, :], (8, 128))
                    picked = jnp.take_along_axis(table, low[:, c:c + 128], axis=1)
                    acc = jnp.where(high[:, c:c + 128] == b, picked, acc)
                for i in range(8):
                    energy[k * 8 + i, :, c:c + 128] = acc[i:i + 1]
        for t in range(OCC):
            column[t] = jnp.transpose(jnp.broadcast_to(energy[row_of(t)], (128, nvir)))
        def flip(t, carry):
            for c in range(pieces):
                own[t, c] = jnp.transpose(
                    parts[t, :, :, :, c * wide:(c + 1) * wide].reshape(n_aux, wide))
            return carry

        lax.fori_loop(0, OCC, flip, 0)

    def densities(amp, run, snap):
        for c in range(pieces):
            def amplitude(n):
                t = slot_ref[0, n]
                ku = slot_ref[1, n]
                ex = jnp.dot(own[t, c], parts[ku].reshape(n_aux, nvir), preferred_element_type=jnp.float32)
                mine = column[t, c * wide:(c + 1) * wide, :]
                denom = (jnp.concatenate([mine] * (nvir // 128), axis=1) + energy[row_of(ku)]
                         - occupied(t) - occupied(ku))
                live = slot_ref[2, n].astype(jnp.float32)
                amp[n % 2] = (ex / denom * live).astype(jnp.bfloat16)

            def contract(n):
                add = lax.dot_general(parts[slot_ref[1, n]].reshape(n_aux, nvir), amp[n % 2], (((1,), (1,)), ((), ())),
                                      preferred_element_type=jnp.float32)
                same = slot_ref[3, n].astype(jnp.float32)
                total = run[...] * same + add
                run[...] = total
                snap[n] = total.astype(jnp.bfloat16)

            run[...] = jnp.zeros_like(run)
            amplitude(0)

            def step(n, carry):
                contract(n - 1)
                amplitude(n)
                return carry

            lax.fori_loop(1, slots, step, 0)
            contract(slots - 1)
            for t in range(OCC):
                some = slot_ref[5, t].astype(jnp.float32).astype(jnp.bfloat16)
                last = snap[slot_ref[4, t]] * some
                for h in range(n_aux // (NQ * BLK)):
                    for p in range(NQ):
                        r0 = (h * NQ + p) * BLK
                        outbox[c, p, t, h] = last[r0:r0 + BLK]
            for d in range(1, NQ):
                send(c, d).start()
            keep_box(c).start()

    mine = pltpu.make_async_copy(
        dom_ref.at[pl.ds(pl.multiple_of(o * doms.shape[0], 8), doms.shape[0])], doms, dsem)
    mine.start()
    for k in range(K):
        names(k).start()

    def collect(raw, xall, ybuf):
        for g in range(rows // 16):
            fetch(g, raw).start()
        regroup(raw, xall)
        mine.wait()
        meet([(peer(q, d), o) for d in range(1, NQ)]
             + [(q, (o + d) % n_occ) for d in range(1, n_occ)])
        for name, r, h in ORDER:
            if name == "transform":
                transform(r, xall, ybuf)
            if name == "select":
                select(r, ybuf)
            if name == "send":
                send_on(r, h)
            if name == "relay":
                relay(r, h)
            if name == "share":
                share(r, h)
            if name == "prepare":
                prepare()

    pl.run_scoped(
        collect,
        pltpu.VMEM((rows // 16, 16, doms.shape[0], nbas), jnp.bfloat16),
        pltpu.VMEM((doms.shape[0], rows, nbas), jnp.bfloat16),
        pltpu.VMEM((NQ, rows, nvall), jnp.bfloat16))
    for r in range(OCC):
        for h in range(2):
            to_core0(r, h).wait_recv()
            share1(r, h).wait_recv()
    pl.run_scoped(
        densities,
        pltpu.VMEM((2, wide, nvir), jnp.bfloat16),
        pltpu.VMEM((n_aux, wide), jnp.float32),
        pltpu.VMEM((slots, n_aux, wide), jnp.bfloat16))
    for c in range(pieces):
        keep_box(c).wait()
        for d in range(1, NQ):
            send(c, d).wait()
    for r in range(OCC):
        for h in range(2):
            for d in range(1, NQ):
                exchange(r, h, d).wait_send()

            @pl.when(core == 0)
            def _():
                around(r, h).wait_send()
                finish_around(r, h).wait_send()
                share0(r, h).wait_send()

            @pl.when(first)
            def _():
                detour(r, h).wait_send()
                finish_detour(r, h).wait_send()

            @pl.when(other)
            def _():
                onward(r, h).wait_send()

            @pl.when(core == 1)
            def _():
                to_core0(r, h).wait_send()
                share1(r, h).wait_send()


def fused(slots, mask, occ, x, coef, dom, vir, pieces):
    rows, local, nbas = x.shape
    nvir = dom.shape[1]
    halves = rows // BLK
    wide = nvir // pieces
    span = K * OCC
    smem = pl.BlockSpec(memory_space=pltpu.SMEM)
    vmem = pl.BlockSpec(memory_space=pltpu.VMEM)
    hbm = pl.BlockSpec(memory_space=pl.ANY)
    dma = pltpu.SemaphoreType.DMA
    unit = (halves, NQ, BLK, nvir)
    box = (pieces, NQ, OCC, halves, BLK, wide)
    return pl.pallas_call(
        fused_kernel,
        out_shape=(jax.ShapeDtypeStruct((NQ, OCC, halves, BLK, nvir), jnp.bfloat16),
                   jax.ShapeDtypeStruct((OCC,) + unit, jnp.bfloat16)),
        in_specs=[smem, smem, smem, hbm, vmem, hbm, vmem],
        out_specs=(hbm, hbm),
        scratch_shapes=[
            pltpu.VMEM((span,) + unit, jnp.bfloat16),
            pltpu.VMEM((OCC,) + unit, jnp.bfloat16),
            pltpu.VMEM(box, jnp.bfloat16),
            pltpu.VMEM((OCC, pieces, wide, NQ * rows), jnp.bfloat16),
            pltpu.VMEM((OCC, nvir, 128), jnp.float32),
            pltpu.VMEM((2 * span, 1, nvir), jnp.float32),
            pltpu.VMEM((256, nvir), jnp.bfloat16),
            pltpu.VMEM((local, nvir), jnp.int32),
            pltpu.VMEM((K, 8, nvir), jnp.int32),
            dma(()), dma((rows // 16,)), dma((OCC, halves)),
            dma((OCC, halves, NQ - 1)), dma((OCC, halves, NQ - 1)),
        ] + [dma((OCC, halves))] * 9 + [
            dma((K,)), dma((pieces,)), dma((pieces, NQ - 1)), dma((pieces, NQ - 1)),
        ],
        compiler_params=pltpu.CompilerParams(collective_id=0, has_side_effects=True,
                                             vmem_limit_bytes=63 << 20),
        name="pair_density",
    )(slots, mask, occ, x, coef, dom, vir)[0]


def slot_kernel(count_ref, code_ref, out_ref):
    span = K * OCC
    cap = code_ref.shape[2]
    count = count_ref[0, 0]

    def clear(n, carry):
        out_ref[0, n] = 0
        out_ref[1, n] = 0
        out_ref[2, n] = 0
        out_ref[3, n] = 0
        return carry

    lax.fori_loop(0, cap, clear, 0)
    at = jnp.int32(0)
    for t in range(OCC):
        begin = at

        def scan(s, n):
            code = code_ref[0, 0, s]
            hit = code // span == t

            @pl.when(hit)
            def _():
                out_ref[0, n] = t
                out_ref[1, n] = code % span
                out_ref[2, n] = 1
                out_ref[3, n] = (n > begin).astype(jnp.int32)
            return n + hit.astype(jnp.int32)

        at = lax.fori_loop(0, count, scan, at)
        out_ref[4, t] = jnp.maximum(at - 1, 0)
        out_ref[5, t] = (at > begin).astype(jnp.int32)


def slot_table(count, codes):
    smem = pl.BlockSpec(memory_space=pltpu.SMEM)
    return pl.pallas_call(
        slot_kernel,
        out_shape=jax.ShapeDtypeStruct((6, codes.shape[2]), jnp.int32),
        in_specs=[smem, smem],
        out_specs=smem,
        name="slot_table",
    )(count, codes)


def body(half_ints, block_mask, vir_coef, domains, vir_energy, occ_energy, pair_count, pair_code):
    rows, local, _ = half_ints.shape
    nvir = domains.shape[1]
    density = fused(slot_table(pair_count, pair_code), block_mask, occ_energy, half_ints,
                    vir_coef, domains, vir_energy.reshape(-1, 128), 2)
    return density.transpose(2, 3, 0, 1, 4).reshape(rows, local, nvir)


def solution(mesh):
    placed = (
        P("aux", "occ", None),
        P("aux", "occ"),
        P(),
        P(),
        P(),
        P(),
        P("occ", "aux"),
        P("occ", "aux", None),
    )
    return jax.shard_map(
        body, mesh=mesh, in_specs=placed, out_specs=P("aux", "occ", None), check_vma=False
    )
```

```python
import functools

import jax
import jax.numpy as jnp
from jax import lax
from jax.experimental import pallas as pl
from jax.experimental.pallas import tpu as pltpu
from jax.sharding import PartitionSpec as P

BLK = 64
OCC = 4
K = 4
NQ = 8
MESH = pl.DeviceIdType.MESH


def timeline():
    steps = []
    for s in range(OCC + 2):
        if s < OCC:
            steps.append(("transform", s, 0))
        if 1 <= s <= OCC:
            steps.append(("send", s - 1, 0))
        if s >= 2:
            steps += [("relay", s - 2, 1), ("share", s - 2, 0)]
        if s < OCC:
            steps.append(("select", s, 0))
        if 1 <= s <= OCC:
            steps += [("relay", s - 1, 0), ("send", s - 1, 1)]
        if s == OCC:
            steps.append(("prepare", 0, 0))
        if s >= 2:
            steps.append(("share", s - 2, 1))
    return steps


ORDER = timeline()


def peer(q, d):
    return (q // 4 + d % 2) % 2 * 4 + (q + d // 2) % 4


def meet(devices):
    barrier = pltpu.get_barrier_semaphore()
    for device in devices:
        pl.semaphore_signal(barrier, inc=1, device_id=device, device_id_type=MESH)
    pl.semaphore_wait(barrier, len(devices))


def fused_kernel(slot_ref, mask_ref, occ_ref, x_ref, coef_ref, dom_ref, vir_ref, out_ref,
                 relay_ref, parts, cbuf, outbox, own, column, energy, ids, doms, near,
                 dsem, xsem, lsem, asend, arecv, bsend, brecv, rsend, rrecv, isend, irecv,
                 fsend, frecv, wsend, nsem, ksem, ssem, dens_sem):
    q = lax.axis_index("aux")
    o = lax.axis_index("occ")
    core = o % 2
    x = (o // 2) % 4
    yl = o // 8
    rows = x_ref.shape[0]
    nbas = x_ref.shape[2]
    nvall = coef_ref.shape[1]
    nvir = parts.shape[-1]
    span = parts.shape[0]
    n_aux = rows * NQ
    n_occ = lax.axis_size("occ")
    low_half = (q % 2) * OCC
    tile = 256
    prev_y = jnp.where(x == 0, 1 - yl, yl)
    relay_y = jnp.where(x >= 2, yl, 1 - yl)
    first = jnp.logical_and(core == 1, x == 0)
    other = jnp.logical_not(first)

    def at(xx, yy, cc):
        return (q, (yy * 4 + xx % 4) * 2 + cc)

    def remote(src, dst, ssem, rsem, dev):
        return pltpu.make_async_remote_copy(
            src_ref=src, dst_ref=dst, send_sem=ssem, recv_sem=rsem,
            device_id=dev, device_id_type=MESH)

    def fetch(g, raw):
        return pltpu.make_async_copy(x_ref.at[pl.ds(g * 16, 16)], raw.at[g], xsem.at[g])

    def exchange(r, h, d):
        to = peer(q, d)
        return remote(cbuf.at[r, h, to], parts.at[r, h, q],
                      asend.at[r, h, d - 1], arecv.at[r, h, d - 1], (to, o))

    def keep(r, h):
        return pltpu.make_async_copy(cbuf.at[r, h, q], parts.at[r, h, q], lsem.at[r, h])

    def onward(r, h):
        return remote(parts.at[r, h], parts.at[2 * OCC + r, h], bsend.at[r, h],
                      brecv.at[r, h], at(x + 3, prev_y, core))

    def detour(r, h):
        return remote(parts.at[r, h], relay_ref.at[r, h], rsend.at[r, h], rrecv.at[r, h],
                      at(0, 1 - yl, 1))

    def around(r, h):
        return remote(parts.at[r, h], relay_ref.at[r, h], rsend.at[r, h], rrecv.at[r, h],
                      at(x + 1, relay_y, 0))

    def to_core0(r, h):
        return remote(parts.at[r, h], parts.at[OCC + r, h], isend.at[r, h],
                      irecv.at[r, h], at(x, yl, 0))

    def share0(r, h):
        return remote(parts.at[2 * OCC + r, h], parts.at[OCC + r, h], fsend.at[r, h],
                      irecv.at[r, h], at(x, yl, 1))

    def share1(r, h):
        return remote(parts.at[2 * OCC + r, h], parts.at[3 * OCC + r, h],
                      fsend.at[r, h], frecv.at[r, h], at(x, yl, 0))

    def finish_around(r, h):
        return remote(relay_ref.at[r, h], parts.at[3 * OCC + r, h], wsend.at[r, h],
                      frecv.at[r, h], at(x + 1, yl, 1))

    def finish_detour(r, h):
        return remote(relay_ref.at[r, h], parts.at[2 * OCC + r, h], wsend.at[r, h],
                      brecv.at[r, h], at(3, yl, 1))

    def regroup(raw, xall):
        size = 8 * NQ * OCC
        row = lax.broadcasted_iota(jnp.int32, (size, size), 0)
        col = lax.broadcasted_iota(jnp.int32, (size, size), 1)
        source = (row % 8) * (NQ * OCC) + ((row // 8) % NQ) * OCC + row // (8 * NQ)
        moved = jnp.where(col == source, 1.0, 0.0).astype(jnp.bfloat16)
        ids[...] = lax.broadcasted_iota(jnp.int32, ids.shape, 0).astype(
            jnp.float32).astype(jnp.bfloat16)

        def group(g, carry):
            fetch(g, raw).wait()
            halves = []
            for half in range(2):
                part = raw[g, 8 * half:8 * half + 8].reshape(size, nbas)
                halves.append(jnp.dot(moved, part, preferred_element_type=jnp.float32)
                              .reshape(NQ * OCC, 8, nbas))
            xall[:, pl.ds(pl.multiple_of(g * 16, 16), 16), :] = jnp.concatenate(
                halves, axis=1).astype(jnp.bfloat16)
            return carry

        lax.fori_loop(0, rows // 16, group, 0)

    def transform(r, xall, ybuf):
        def columns(n, carry):
            c0 = pl.multiple_of(n * tile, tile)
            for h in range(2):
                half = NQ // 2
                g0 = r * NQ + half * h
                part = xall[g0:g0 + half].reshape(half * rows, nbas)
                y = jnp.dot(part, coef_ref[:, pl.ds(c0, tile)],
                            preferred_element_type=jnp.float32)
                ybuf[half * h:half * (h + 1), :, pl.ds(c0, tile)] = y.astype(
                    jnp.bfloat16).reshape(half, rows, tile)
            return carry

        lax.fori_loop(0, nvall // tile, columns, 0)

    def select(r, ybuf):
        def depart(d):
            @pl.when(d > 0)
            def _():
                exchange(r, 0, d).start()

            @pl.when(d == 0)
            def _():
                keep(r, 0).start()

        def orbital(d, carry):
            g = peer(q, d)
            dom = doms[pl.ds(g * OCC + r, 1), :]
            hot = []
            for n in range(nvall // tile):
                near = dom - n * tile
                inside = jnp.logical_and(near >= 0, near < tile)
                near = jnp.where(inside, near, -1).astype(jnp.float32).astype(jnp.bfloat16)
                hot.append(jnp.where(ids[...] == near, jnp.bfloat16(1), jnp.bfloat16(0)))
            acc = jnp.dot(ybuf[g], jnp.concatenate(hot, axis=0),
                          preferred_element_type=jnp.float32)
            for b in range(rows // BLK):
                m = mask_ref[b, g * OCC + r].astype(jnp.float32)
                cbuf[r, b, g] = (acc[b * BLK:(b + 1) * BLK] * m).astype(jnp.bfloat16)

            @pl.when(d > 0)
            def _():
                depart(d - 1)
            return carry

        lax.fori_loop(0, NQ, orbital, 0)
        depart(NQ - 1)
        for d in range(1, NQ):
            exchange(r, 1, d).start()
        keep(r, 1).start()

    def send_on(r, h):
        keep(r, h).wait()
        for d in range(1, NQ):
            exchange(r, h, d).wait_recv()

        @pl.when(core == 0)
        def _():
            around(r, h).start()

        @pl.when(first)
        def _():
            detour(r, h).start()

        @pl.when(other)
        def _():
            onward(r, h).start()

        @pl.when(core == 1)
        def _():
            to_core0(r, h).start()

    def relay(r, h):
        @pl.when(core == 0)
        def _():
            around(r, h).wait_recv()
            finish_around(r, h).start()

        @pl.when(first)
        def _():
            detour(r, h).wait_recv()
            finish_detour(r, h).start()

    def share(r, h):
        onward(r, h).wait_recv()

        @pl.when(core == 0)
        def _():
            share0(r, h).start()

        @pl.when(core == 1)
        def _():
            share1(r, h).start()

    pieces = outbox.shape[0]
    wide = nvir // pieces
    slots = slot_ref.shape[1]

    def landing(c):
        return out_ref.at[q, :, :, :, pl.ds(c * wide, wide)]

    def row_of(ku):
        return (ku // OCC) * 8 + low_half + ku % OCC

    def occupied(ku):
        return occ_ref[((o + ku // OCC) % n_occ * NQ + q) * OCC + ku % OCC]

    def names(k):
        first = ((o + k) % n_occ * NQ + q) // 2 * 8
        return pltpu.make_async_copy(dom_ref.at[pl.ds(pl.multiple_of(first, 8), 8)],
                                     near.at[k], nsem.at[k])

    def send(c, d):
        to = peer(q, d)
        return pltpu.make_async_remote_copy(
            src_ref=outbox.at[c, to], dst_ref=landing(c), send_sem=ssem.at[c, d - 1],
            recv_sem=dens_sem.at[c, d - 1], device_id=(to, o), device_id_type=MESH)

    def keep_box(c):
        return pltpu.make_async_copy(outbox.at[c, q], landing(c), ksem.at[c])

    def prepare():
        for k in range(K):
            names(k).wait()
            low = near[k] % 128
            high = near[k] // 128
            for c in range(0, nvir, 128):
                acc = jnp.zeros((8, 128), jnp.float32)
                for b in range(vir_ref.shape[0]):
                    table = jnp.broadcast_to(vir_ref[b:b + 1, :], (8, 128))
                    picked = jnp.take_along_axis(table, low[:, c:c + 128], axis=1)
                    acc = jnp.where(high[:, c:c + 128] == b, picked, acc)
                for i in range(8):
                    energy[k * 8 + i, :, c:c + 128] = acc[i:i + 1]
        for t in range(OCC):
            column[t] = jnp.transpose(jnp.broadcast_to(energy[row_of(t)], (128, nvir)))
        def flip(t, carry):
            for c in range(pieces):
                own[t, c] = jnp.transpose(
                    parts[t, :, :, :, c * wide:(c + 1) * wide].reshape(n_aux, wide))
            return carry

        lax.fori_loop(0, OCC, flip, 0)

    def densities(amp, run, snap):
        for c in range(pieces):
            def amplitude(n):
                t = slot_ref[0, n]
                ku = slot_ref[1, n]
                ex = jnp.dot(own[t, c], parts[ku].reshape(n_aux, nvir), preferred_element_type=jnp.float32)
                mine = column[t, c * wide:(c + 1) * wide, :]
                denom = (jnp.concatenate([mine] * (nvir // 128), axis=1) + energy[row_of(ku)]
                         - occupied(t) - occupied(ku))
                live = slot_ref[2, n].astype(jnp.float32)
                amp[n % 2] = (ex / denom * live).astype(jnp.bfloat16)

            def contract(n):
                add = lax.dot_general(parts[slot_ref[1, n]].reshape(n_aux, nvir), amp[n % 2], (((1,), (1,)), ((), ())),
                                      preferred_element_type=jnp.float32)
                same = slot_ref[3, n].astype(jnp.float32)
                total = run[...] * same + add
                run[...] = total
                snap[n] = total.astype(jnp.bfloat16)

            run[...] = jnp.zeros_like(run)
            amplitude(0)

            def step(n, carry):
                contract(n - 1)
                amplitude(n)
                return carry

            lax.fori_loop(1, slots, step, 0)
            contract(slots - 1)
            for t in range(OCC):
                some = slot_ref[5, t].astype(jnp.float32).astype(jnp.bfloat16)
                last = snap[slot_ref[4, t]] * some
                for h in range(n_aux // (NQ * BLK)):
                    for p in range(NQ):
                        r0 = (h * NQ + p) * BLK
                        outbox[c, p, t, h] = last[r0:r0 + BLK]
            for d in range(1, NQ):
                send(c, d).start()
            keep_box(c).start()

    mine = pltpu.make_async_copy(
        dom_ref.at[pl.ds(pl.multiple_of(o * doms.shape[0], 8), doms.shape[0])], doms, dsem)
    mine.start()
    for k in range(K):
        names(k).start()

    def collect(raw, xall, ybuf):
        for g in range(rows // 16):
            fetch(g, raw).start()
        regroup(raw, xall)
        mine.wait()
        meet([(peer(q, d), o) for d in range(1, NQ)]
             + [(q, (o + d) % n_occ) for d in range(1, n_occ)])
        for name, r, h in ORDER:
            if name == "transform":
                transform(r, xall, ybuf)
            if name == "select":
                select(r, ybuf)
            if name == "send":
                send_on(r, h)
            if name == "relay":
                relay(r, h)
            if name == "share":
                share(r, h)
            if name == "prepare":
                prepare()

    pl.run_scoped(
        collect,
        pltpu.VMEM((rows // 16, 16, doms.shape[0], nbas), jnp.bfloat16),
        pltpu.VMEM((doms.shape[0], rows, nbas), jnp.bfloat16),
        pltpu.VMEM((NQ, rows, nvall), jnp.bfloat16))
    for r in range(OCC):
        for h in range(2):
            to_core0(r, h).wait_recv()
            share1(r, h).wait_recv()
    pl.run_scoped(
        densities,
        pltpu.VMEM((2, wide, nvir), jnp.bfloat16),
        pltpu.VMEM((n_aux, wide), jnp.float32),
        pltpu.VMEM((slots, n_aux, wide), jnp.bfloat16))
    for c in range(pieces):
        keep_box(c).wait()
        for d in range(1, NQ):
            send(c, d).wait()
    for r in range(OCC):
        for h in range(2):
            for d in range(1, NQ):
                exchange(r, h, d).wait_send()

            @pl.when(core == 0)
            def _():
                around(r, h).wait_send()
                finish_around(r, h).wait_send()
                share0(r, h).wait_send()

            @pl.when(first)
            def _():
                detour(r, h).wait_send()
                finish_detour(r, h).wait_send()

            @pl.when(other)
            def _():
                onward(r, h).wait_send()

            @pl.when(core == 1)
            def _():
                to_core0(r, h).wait_send()
                share1(r, h).wait_send()


def fused(slots, mask, occ, x, coef, dom, vir, pieces):
    rows, local, nbas = x.shape
    nvir = dom.shape[1]
    halves = rows // BLK
    wide = nvir // pieces
    span = K * OCC
    smem = pl.BlockSpec(memory_space=pltpu.SMEM)
    vmem = pl.BlockSpec(memory_space=pltpu.VMEM)
    hbm = pl.BlockSpec(memory_space=pl.ANY)
    dma = pltpu.SemaphoreType.DMA
    unit = (halves, NQ, BLK, nvir)
    box = (pieces, NQ, OCC, halves, BLK, wide)
    return pl.pallas_call(
        fused_kernel,
        out_shape=(jax.ShapeDtypeStruct((NQ, OCC, halves, BLK, nvir), jnp.bfloat16),
                   jax.ShapeDtypeStruct((OCC,) + unit, jnp.bfloat16)),
        in_specs=[smem, smem, smem, hbm, vmem, hbm, vmem],
        out_specs=(hbm, hbm),
        scratch_shapes=[
            pltpu.VMEM((span,) + unit, jnp.bfloat16),
            pltpu.VMEM((OCC,) + unit, jnp.bfloat16),
            pltpu.VMEM(box, jnp.bfloat16),
            pltpu.VMEM((OCC, pieces, wide, NQ * rows), jnp.bfloat16),
            pltpu.VMEM((OCC, nvir, 128), jnp.float32),
            pltpu.VMEM((2 * span, 1, nvir), jnp.float32),
            pltpu.VMEM((256, nvir), jnp.bfloat16),
            pltpu.VMEM((local, nvir), jnp.int32),
            pltpu.VMEM((K, 8, nvir), jnp.int32),
            dma(()), dma((rows // 16,)), dma((OCC, halves)),
            dma((OCC, halves, NQ - 1)), dma((OCC, halves, NQ - 1)),
        ] + [dma((OCC, halves))] * 9 + [
            dma((K,)), dma((pieces,)), dma((pieces, NQ - 1)), dma((pieces, NQ - 1)),
        ],
        compiler_params=pltpu.CompilerParams(collective_id=0, has_side_effects=True,
                                             vmem_limit_bytes=63 << 20),
        name="pair_density",
    )(slots, mask, occ, x, coef, dom, vir)[0]


def slot_kernel(count_ref, code_ref, out_ref):
    span = K * OCC
    cap = code_ref.shape[2]
    count = count_ref[0, 0]

    def clear(n, carry):
        out_ref[0, n] = 0
        out_ref[1, n] = 0
        out_ref[2, n] = 0
        out_ref[3, n] = 0
        return carry

    lax.fori_loop(0, cap, clear, 0)
    at = jnp.int32(0)
    for t in range(OCC):
        begin = at

        def scan(s, n):
            code = code_ref[0, 0, s]
            hit = code // span == t

            @pl.when(hit)
            def _():
                out_ref[0, n] = t
                out_ref[1, n] = code % span
                out_ref[2, n] = 1
                out_ref[3, n] = (n > begin).astype(jnp.int32)
            return n + hit.astype(jnp.int32)

        at = lax.fori_loop(0, count, scan, at)
        out_ref[4, t] = jnp.maximum(at - 1, 0)
        out_ref[5, t] = (at > begin).astype(jnp.int32)


def slot_table(count, codes):
    smem = pl.BlockSpec(memory_space=pltpu.SMEM)
    return pl.pallas_call(
        slot_kernel,
        out_shape=jax.ShapeDtypeStruct((6, codes.shape[2]), jnp.int32),
        in_specs=[smem, smem],
        out_specs=smem,
        name="slot_table",
    )(count, codes)


def body(half_ints, block_mask, vir_coef, domains, vir_energy, occ_energy, pair_count, pair_code):
    rows, local, _ = half_ints.shape
    nvir = domains.shape[1]
    density = fused(slot_table(pair_count, pair_code), block_mask, occ_energy, half_ints,
                    vir_coef, domains, vir_energy.reshape(-1, 128), 2)
    return density.transpose(2, 3, 0, 1, 4).reshape(rows, local, nvir)


def solution(mesh):
    placed = (
        P("aux", "occ", None),
        P("aux", "occ"),
        P(),
        P(),
        P(),
        P(),
        P("occ", "aux"),
        P("occ", "aux", None),
    )
    return jax.shard_map(
        body, mesh=mesh, in_specs=placed, out_specs=P("aux", "occ", None), check_vma=False
    )
```
